32 devices in a mesh: sec: 8 (over z, x), row: 4 (over y, core).
Axes of the slice: x: 2, y: 2, z: 4, core: 2. Of those that a mesh axis runs over, the one named last changes fastest.
Arguments:
- left_block: bfloat16 [16, 2048, 128], P('sec', 'row'), may hold values from -6 to 6
- right_block: bfloat16 [16, 128, 2048], P('sec'), may hold values from -6 to 6
- left_ops: float32 [4, 16, 16], replicated, may hold values from -1.5 to 1.5
- right_ops: float32 [4, 16, 16], replicated, may hold values from -1.5 to 1.5
- charges: int32 [16], replicated, may hold values from 0 to 6
- live_states: int32 [16], replicated, may hold values from 64 to 128
- kept: int32 [16], replicated, may hold values from 64 to 128
- start: int32 [16, 128], replicated, may hold values from 0 to 511, all different within a row
Outputs:
- basis: float32 [16, 2048, 128], P('sec', 'row')
- right_new: float32 [16, 128, 2048], P('sec', None, 'row')
The draws below stay inside these ranges and needn't reach their ends.
Inputs may be any that keep to these rules, and one draw needn't show every extreme that they name: The 128 start columns of a sector are distinct.
All inputs are finite; a program needn't handle non-finite values.
Results may differ from the reference program's by a relative error of at most 0.0065.
Values may be sent and summed in bfloat16 or wider, within the bound.
A program may use at most 64 MiB of HBM per device.

```python
import jax
import jax.numpy as jnp
from jax import lax

SITE = 16
STATES = 128
KEEP = 128
TERMS = 4
ITERS = 2
SECTORS = 16
ROWS = 2048
COLS = 2048


def set_ends(result, stream_key, least, top_value):
    place = [jax.random.randint(jax.random.fold_in(stream_key, axis), (), 0, length) for axis, length in enumerate(result.shape)]
    widest = result.shape.index(max(result.shape))
    neighbour = place[:widest] + [(place[widest] + 1) % result.shape[widest]] + place[widest + 1:]
    return result.at[tuple(place)].set(least).at[tuple(neighbour)].set(top_value)


def levels(stream_key, shape, shards, smallest, largest):
    factor_of, own = 1.0, jax.random.fold_in(stream_key, 6)
    for dim, shards_of in shards:
        draws = jnp.exp(jax.random.uniform(jax.random.fold_in(own, dim), (shards_of,), jnp.float32, smallest / len(shards), largest / len(shards)))
        factor_of = factor_of * jnp.repeat(draws, shape[dim] // shards_of).reshape([-1 if axis == dim else 1 for axis in range(len(shape))])
    return factor_of


def different_ones(stream_key, rows, count, top, lift):
    ranking = jax.random.permutation(jax.random.fold_in(stream_key, 1), count)
    favour = ranking
    for power in range(3):
        favour = favour * favour // count
    favour = favour * lift // count
    tickets = jax.random.randint(jax.random.fold_in(stream_key, 2), (rows, count), 0, 4096) + favour
    holders = jax.random.permutation(jax.random.fold_in(stream_key, 3), rows)[jnp.arange(count) % rows]
    tickets = jnp.where(jnp.arange(rows)[:, None] == holders[None, :], 1 << 14, tickets)
    score = tickets * count + jnp.arange(count)
    return lax.top_k(score.astype(jnp.int32), top)[1].astype(jnp.int32)


def noise(own_key, shape, spread, reach, shards=(), kind=jnp.bfloat16):
    factor_of = levels(own_key, shape, shards, -0.22, 0.18) if shards else 1.0
    values = jax.random.normal(own_key, shape, jnp.float32) * spread * factor_of
    return jnp.minimum(jnp.maximum(values, -reach), reach).astype(kind)


def setup_inputs(seed: int = 0) -> dict:
    keys = jax.random.split(jax.random.key(seed), 9)
    return {
        "left_block": noise(keys[0], (SECTORS, ROWS, STATES), 1.0, 6.0, ((0, 8), (1, 4))),
        "right_block": noise(keys[1], (SECTORS, STATES, COLS), 1.0, 6.0, ((0, 8),)),
        "left_ops": noise(keys[2], (TERMS, SITE, SITE), SITE ** -0.5, 1.5, (), jnp.float32),
        "right_ops": noise(keys[3], (TERMS, SITE, SITE), SITE ** -0.5, 1.5, (), jnp.float32),
        "charges": set_ends(jax.random.randint(keys[4], (SECTORS,), 0, 7), jax.random.fold_in(keys[4], 1), 0, 6).astype(jnp.int32),
        "live_states": set_ends(jax.random.randint(keys[5], (SECTORS,), STATES // 2, STATES + 1), jax.random.fold_in(keys[5], 1), STATES // 2, STATES).astype(jnp.int32),
        "kept": set_ends(jax.random.randint(keys[6], (SECTORS,), KEEP // 2, KEEP + 1), jax.random.fold_in(keys[6], 1), KEEP // 2, KEEP).astype(jnp.int32),
        "start": different_ones(keys[7], SECTORS, TERMS * STATES, KEEP, 0),
    }


chemical = 0.4
highest = lax.Precision.HIGHEST

def gate_rows(tensor_block, operators):
    site_dim = operators.shape[1]
    grouped = tensor_block.astype(jnp.float32).reshape(tensor_block.shape[0] // site_dim, site_dim, tensor_block.shape[1])
    mixed_rows = jnp.einsum('tij,ajk->aitk', operators.astype(jnp.float32), grouped, precision=highest)
    return mixed_rows.reshape(tensor_block.shape[0], operators.shape[0] * tensor_block.shape[1]).astype(jnp.bfloat16)

def gate_columns(tensor_block, operators):
    site_dim = operators.shape[1]
    grouped = tensor_block.astype(jnp.float32).reshape(tensor_block.shape[0], site_dim, tensor_block.shape[1] // site_dim)
    mixed_columns = jnp.einsum('tij,kjb->tkib', operators.astype(jnp.float32), grouped, precision=highest)
    return mixed_columns.reshape(operators.shape[0] * tensor_block.shape[0], tensor_block.shape[1]).astype(jnp.bfloat16)

def orthonormal(krylov):
    gram_matrix = jnp.dot(krylov.T, krylov, precision=highest)
    factor = jnp.linalg.cholesky(gram_matrix)
    return jax.scipy.linalg.solve_triangular(factor, krylov.T, lower=True).T

def reference(left_block, right_block, left_ops, right_ops, charges, live_states, kept, start):
    half_count = SECTORS // 2

    def one_sector(packed):
        left_tensor, right_tensor, live_count, charge_value, kept_count, columns = packed
        row_states = jnp.arange(left_tensor.shape[0], dtype=jnp.int32) // SITE
        left_masked = jnp.where((row_states < live_count)[:, None], left_tensor, jnp.zeros((), jnp.bfloat16))
        left_gated = gate_rows(left_masked, left_ops)
        right_gated = gate_columns(right_tensor, right_ops)
        weight = jnp.exp(-chemical * charge_value.astype(jnp.float32))
        theta_block = weight * jnp.dot(left_gated.astype(jnp.float32), right_gated.astype(jnp.float32), preferred_element_type=jnp.float32)
        krylov = jnp.take(left_gated, columns, axis=1).astype(jnp.float32)
        for round_index in range(ITERS):
            ortho_block = orthonormal(krylov)
            projected = jnp.dot(theta_block.T, ortho_block, precision=highest)
            krylov = jnp.dot(theta_block, projected, precision=highest)
        ortho_block = orthonormal(krylov)
        right_part = jnp.dot(ortho_block.T, theta_block, precision=highest)
        keep_mask = (jnp.arange(KEEP, dtype=jnp.int32) < kept_count).astype(jnp.float32)
        return (ortho_block * keep_mask[None, :], right_part * keep_mask[:, None])
    paired = (left_block, jnp.roll(right_block, -half_count, axis=0), live_states, jnp.roll(charges, -half_count), jnp.roll(kept, -half_count), start)
    basis_all, right_all = lax.map(one_sector, paired)
    total_weight = jnp.sum(right_all * right_all)
    right_all = right_all / jnp.sqrt(total_weight)
    return (basis_all, jnp.roll(right_all, half_count, axis=0))
```

```python
import functools

import jax
import jax.numpy as jnp
from jax import lax
from jax.experimental import pallas as pl
from jax.experimental.pallas import tpu as pltpu
from jax.sharding import PartitionSpec as P

MESH = pl.DeviceIdType.MESH
HIGHEST = lax.Precision.HIGHEST
F32, BF16 = jnp.float32, jnp.bfloat16
chemical = 0.4
ITERS = 2
PANEL = 16
VM = pl.BlockSpec(memory_space=pltpu.VMEM)
SM = pl.BlockSpec(memory_space=pltpu.SMEM)


def nn(a, b, precision=None):
    return lax.dot_general(
        a, b, (((1,), (0,)), ((), ())), precision=precision, preferred_element_type=F32
    )


def nt(a, b, precision=None):
    return lax.dot_general(
        a, b, (((1,), (1,)), ((), ())), precision=precision, preferred_element_type=F32
    )


def tn(a, b, precision=None):
    return lax.dot_general(
        a, b, (((0,), (0,)), ((), ())), precision=precision, preferred_element_type=F32
    )


def split2(x):
    high = x.astype(BF16)
    return high, (x - high.astype(F32)).astype(BF16)


def split3(x):
    high, rest = x.astype(BF16), None
    rest = x - high.astype(F32)
    mid = rest.astype(BF16)
    return high, mid, (rest - mid.astype(F32)).astype(BF16)


def iota(shape, dim):
    return lax.broadcasted_iota(jnp.int32, shape, dim)


def exchange_kernel(row_count, mask, left_ref, right_ref, left_out, right_out, send, recv):
    row, sec = lax.axis_index("row"), lax.axis_index("sec")
    rows = left_ref.shape[1]
    depth = right_ref.shape[1] // row_count

    def peer_row(distance):
        return (sec, jnp.bitwise_xor(row, distance))

    partner = (jnp.bitwise_xor(sec, mask), row)
    distances = []
    step = row_count // 2
    while step:
        distances.append(step)
        step //= 2
    barrier = pltpu.get_barrier_semaphore()
    for device in [partner] + [peer_row(d) for d in distances]:
        pl.semaphore_signal(barrier, inc=1, device_id=device, device_id_type=MESH)
    pl.semaphore_wait(barrier, 1 + len(distances))

    def left_at(owner):
        return left_out.at[:, pl.ds(pl.multiple_of(owner * rows, rows), rows), :]

    def right_at(ref, owner):
        return ref.at[:, pl.ds(pl.multiple_of(owner * depth, depth), depth), :]

    copies = []

    def go(source, target, device):
        index = len(copies)
        copy = pltpu.make_async_remote_copy(
            src_ref=source, dst_ref=target, send_sem=send.at[index], recv_sem=recv.at[index],
            device_id=device, device_id_type=MESH,
        )
        copy.start()
        copies.append(copy)
        return copy

    taken = []

    def arrive(copy):
        if copy is not None and id(copy) not in taken:
            copy.wait_recv()
            taken.append(id(copy))

    first = go(right_at(right_ref, row), right_at(right_out, row), partner)
    held = [(row, None)]
    for distance in distances:
        sent = []
        for owner, copy in held:
            arrive(copy)
            source = left_ref if copy is None else left_at(owner)
            sent.append(
                (jnp.bitwise_xor(owner, distance), go(source, left_at(owner), peer_row(distance)))
            )
        held = held + sent
    own = pl.ds(pl.multiple_of(row * rows, rows), rows)
    left_out[:, own, :] = left_ref[...]
    held = [(row, first)]
    for distance in distances:
        sent = []
        for owner, copy in held:
            arrive(copy)
            block = right_at(right_out, owner)
            sent.append((jnp.bitwise_xor(owner, distance), go(block, block, peer_row(distance))))
        held = held + sent
    for copy in copies:
        copy.wait_send()
        arrive(copy)


def exchange(row_count, sec_count, left, right):
    slots, rows, states = left.shape
    count = 2 * (row_count - 1) + 1
    return pl.pallas_call(
        functools.partial(exchange_kernel, row_count, sec_count // 2),
        out_shape=(
            jax.ShapeDtypeStruct((slots, rows * row_count, states), left.dtype),
            jax.ShapeDtypeStruct(right.shape, right.dtype),
        ),
        in_specs=[VM] * 2,
        out_specs=[VM] * 2,
        scratch_shapes=[pltpu.SemaphoreType.DMA((count,)), pltpu.SemaphoreType.DMA((count,))],
        compiler_params=pltpu.CompilerParams(collective_id=0, has_side_effects=True),
    )(left, right)


def spread(ops, row_of, col_of, same):
    site = ops.shape[0]
    pick_rows = (iota((row_of.shape[0], site), 1) == row_of).astype(BF16)
    pick_cols = (iota((site, col_of.shape[1]), 0) == col_of).astype(BF16)
    out = []
    for part in split2(ops):
        wide = nn(nn(pick_rows, part).astype(BF16), pick_cols)
        out.append(jnp.where(same, wide, 0.0).astype(BF16))
    return out


def inverse_factor(grams, s_ref, t_ref):
    size = grams[0].shape[0]
    slots = len(grams)
    eye = (iota((size, size), 0) == iota((size, size), 1)).astype(F32)
    for s in range(slots):
        s_ref[s] = grams[s]
        t_ref[s] = eye
    sub = iota((PANEL, size), 0)
    lane = iota((PANEL, size), 1)

    def panel(p, carry):
        base = pl.multiple_of(p * PANEL, PANEL)
        for s in range(slots):
            upper = s_ref[s, pl.ds(base, PANEL), :]
            lower = t_ref[s, pl.ds(base, PANEL), :]
            turned = pltpu.roll(upper, lax.rem(size - base, size), 1)
            cols = [jnp.broadcast_to(turned[:, c : c + 1], (PANEL, size)) for c in range(PANEL)]
            for j in range(PANEL):
                scale = lax.rsqrt(cols[j][j : j + 1, :])
                below = jnp.where(sub > j, cols[j] * scale, 0.0)
                at_j = sub == j

                def eliminate(x):
                    pivot = x[j : j + 1, :] * scale
                    return jnp.where(at_j, pivot, x - below * pivot)

                upper, lower = eliminate(upper), eliminate(lower)
                cols = [eliminate(c) if i > j else c for i, c in enumerate(cols)]
            t_ref[s, pl.ds(base, PANEL), :] = lower
            u3, l3 = split3(upper), split3(lower)
            later = lane >= base + PANEL
            m3 = [jnp.where(later, x.astype(F32), 0.0).astype(BF16) for x in u3]
            pairs = ((0, 0), (0, 1), (1, 0), (1, 1), (0, 2), (2, 0))
            lhs = jnp.concatenate([m3[i] for i, _ in pairs], axis=0)
            rhs = jnp.concatenate(
                [jnp.concatenate([u3[k], l3[k]], axis=1) for _, k in pairs], axis=0
            )
            change = tn(lhs, rhs)
            s_ref[s] = s_ref[s] - change[:, :size]
            t_ref[s] = t_ref[s] - change[:, size:]
        return carry

    lax.fori_loop(0, size // PANEL, panel, 0)


def chain_kernel(
    sector_count, left_ref, right_ref, lops_ref, rops_ref, charges_ref, live_ref, kept_ref,
    start_ref, m_out, u_out, part_out, at_ref, b_ref, kl_ref, kr_ref, ga_ref, gb_ref, s_ref,
    t_ref,
):
    slots, rows, states = left_ref.shape
    terms, site = lops_ref.shape[0], lops_ref.shape[1]
    cols = right_ref.shape[2]
    width = cols // site
    group = 256 // site
    block = group * site
    sec, row = lax.axis_index("sec"), lax.axis_index("row")
    homes = [sec * slots + s for s in range(slots)]
    mirrors = [lax.rem(h + sector_count // 2, sector_count) for h in homes]
    r0, c0 = iota((block, 1), 0), iota((1, block), 1)
    for t in range(terms):
        parts = spread(lops_ref[t].T, r0 % site, c0 % site, (r0 // site) == (c0 // site))
        for h in range(2):
            kl_ref[h, :, t * block : (t + 1) * block] = parts[h]
        parts = spread(rops_ref[t], r0 // group, c0 // group, (r0 % group) == (c0 % group))
        for h in range(2):
            kr_ref[h, t * block : (t + 1) * block, :] = parts[h]
    for s in range(slots):
        limit = live_ref[homes[s]] * site

        def left_chunk(c, carry):
            base = pl.multiple_of(c * block, block)
            piece = left_ref[s, pl.ds(base, block), :]
            piece = jnp.where(iota((block, states), 0) + base < limit, piece.astype(F32), 0.0)
            turned = piece.T.astype(BF16)
            out = nn(turned, kl_ref[0]) + nn(turned, kl_ref[1])
            for t in range(terms):
                at_ref[s, t * states : (t + 1) * states, pl.ds(base, block)] = out[
                    :, t * block : (t + 1) * block
                ].astype(BF16)
            return carry

        lax.fori_loop(0, rows // block, left_chunk, 0)

        def right_chunk(c, carry):
            base = pl.multiple_of(c * group, group)
            piece = right_ref[s, pl.ds(base, group), :]
            stack = jnp.concatenate([piece[:, j * width : (j + 1) * width] for j in range(site)], axis=0)
            out = (nn(kr_ref[0], stack) + nn(kr_ref[1], stack)).astype(BF16)
            for t in range(terms):
                for i in range(site):
                    b_ref[
                        s, pl.ds(t * states + base, group), i * width : (i + 1) * width
                    ] = out[t * block + i * group : t * block + (i + 1) * group, :]
            return carry

        lax.fori_loop(0, states // group, right_chunk, 0)
        ga_ref[s] = nt(at_ref[s], at_ref[s])
        gb_ref[s] = nt(b_ref[s], b_ref[s])

    bond = terms * states
    weights = [
        jnp.exp(jnp.full((1, states), charges_ref[m], jnp.int32).astype(F32) * (-chemical))
        for m in mirrors
    ]
    coef = []
    for s in range(slots):
        wanted = start_ref[pl.ds(homes[s], 1), :]
        coef.append((iota((bond, wanted.shape[1]), 0) == wanted).astype(F32))
    for round_index in range(ITERS + 1):
        image = [nn(ga_ref[s], coef[s], HIGHEST) for s in range(slots)]
        inverse_factor([tn(coef[s], image[s], HIGHEST) for s in range(slots)], s_ref, t_ref)
        image = [nt(image[s], t_ref[s], HIGHEST) for s in range(slots)]
        if round_index < ITERS:
            coef = [
                nn(gb_ref[s], image[s], HIGHEST) * (weights[s] * weights[s]) for s in range(slots)
            ]
        else:
            coef = [nt(coef[s], t_ref[s], HIGHEST) for s in range(slots)]
    local_rows = u_out.shape[1]
    total = jnp.zeros((8, states), F32)
    for s in range(slots):
        keep = iota((bond, coef[s].shape[1]), 1) < kept_ref[mirrors[s]]
        out = jnp.where(keep, image[s] * weights[s], 0.0)
        m_out[s] = out.astype(BF16)
        per = out * nn(gb_ref[s], out, HIGHEST)
        total = total + jnp.sum(per.reshape(bond // 8, 8, per.shape[1]), axis=0)
        high, low = split2(jnp.where(keep, coef[s], 0.0))
        here = at_ref[s, :, pl.ds(pl.multiple_of(row * local_rows, local_rows), local_rows)]
        u_out[s] = tn(here, high) + tn(here, low)
    part_out[...] = total


def chain(sector_count, left, right, lops, rops, charges, live, kept, start, local_rows):
    slots, rows, states = left.shape
    terms, site = lops.shape[0], lops.shape[1]
    cols, bond, keep = right.shape[2], terms * states, start.shape[1]
    block = 256
    return pl.pallas_call(
        functools.partial(chain_kernel, sector_count),
        out_shape=(
            jax.ShapeDtypeStruct((slots, bond, keep), BF16),
            jax.ShapeDtypeStruct((slots, local_rows, keep), F32),
            jax.ShapeDtypeStruct((8, keep), F32),
        ),
        in_specs=[VM] * 4 + [SM] * 3 + [VM],
        out_specs=[VM] * 3,
        scratch_shapes=[
            pltpu.VMEM((slots, bond, rows), BF16),
            pltpu.VMEM((slots, bond, cols), BF16),
            pltpu.VMEM((2, block, terms * block), BF16),
            pltpu.VMEM((2, terms * block, block), BF16),
            pltpu.VMEM((slots, bond, bond), F32),
            pltpu.VMEM((slots, bond, bond), F32),
            pltpu.VMEM((slots, keep, keep), F32),
            pltpu.VMEM((slots, keep, keep), F32),
        ],
        compiler_params=pltpu.CompilerParams(vmem_limit_bytes=56 * 2**20),
    )(left, right, lops, rops, charges, live, kept, start)


def deliver_kernel(sec_count, m_ref, part_ref, m_out, parts_out, m_send, m_recv, send, recv):
    row, sec = lax.axis_index("row"), lax.axis_index("sec")
    partner = (jnp.bitwise_xor(sec, sec_count // 2), row)
    barrier = pltpu.get_barrier_semaphore()
    for d in range(1, sec_count):
        pl.semaphore_signal(
            barrier, inc=1, device_id=(jnp.bitwise_xor(sec, d), row), device_id_type=MESH
        )
    pl.semaphore_wait(barrier, sec_count - 1)
    small = []
    for d in range(1, sec_count):
        copy = pltpu.make_async_remote_copy(
            src_ref=part_ref, dst_ref=parts_out.at[d], send_sem=send.at[d], recv_sem=recv.at[d],
            device_id=(jnp.bitwise_xor(sec, d), row), device_id_type=MESH,
        )
        copy.start()
        small.append(copy)
    big = pltpu.make_async_remote_copy(
        src_ref=m_ref, dst_ref=m_out, send_sem=m_send, recv_sem=m_recv, device_id=partner,
        device_id_type=MESH,
    )
    big.start()
    parts_out[0] = part_ref[...]
    for copy in small:
        copy.wait()
    big.wait()


def deliver(sec_count, m, part):
    return pl.pallas_call(
        functools.partial(deliver_kernel, sec_count),
        out_shape=(
            jax.ShapeDtypeStruct(m.shape, m.dtype),
            jax.ShapeDtypeStruct((sec_count,) + part.shape, part.dtype),
        ),
        in_specs=[VM] * 2,
        out_specs=[VM] * 2,
        scratch_shapes=[
            pltpu.SemaphoreType.DMA,
            pltpu.SemaphoreType.DMA,
            pltpu.SemaphoreType.DMA((sec_count,)),
            pltpu.SemaphoreType.DMA((sec_count,)),
        ],
        compiler_params=pltpu.CompilerParams(collective_id=1, has_side_effects=True),
    )(m, part)


def finish_kernel(row_count, m_ref, parts_ref, right_ref, rops_ref, out_ref, kr_ref, b_ref):
    slots, states, cols = right_ref.shape
    terms, site = rops_ref.shape[0], rops_ref.shape[1]
    width = cols // site
    group = 256 // site
    block = group * site
    here = site // row_count
    part_rows = here * group
    row = lax.axis_index("row")
    r0, c0 = iota((part_rows, 1), 0), iota((1, block), 1)
    for t in range(terms):
        parts = spread(
            rops_ref[t], row * here + r0 // group, c0 // group, (r0 % group) == (c0 % group)
        )
        for h in range(2):
            kr_ref[h, t * part_rows : (t + 1) * part_rows, :] = parts[h]
    total = jnp.sum(jnp.sum(parts_ref[...], axis=0), keepdims=True)
    scale = 1.0 / jnp.sqrt(total)
    for s in range(slots):
        def right_chunk(c, carry):
            base = pl.multiple_of(c * group, group)
            piece = right_ref[s, pl.ds(base, group), :]
            stack = jnp.concatenate([piece[:, j * width : (j + 1) * width] for j in range(site)], axis=0)
            out = (nn(kr_ref[0], stack) + nn(kr_ref[1], stack)).astype(BF16)
            for t in range(terms):
                for i in range(here):
                    b_ref[pl.ds(t * states + base, group), i * width : (i + 1) * width] = out[
                        t * part_rows + i * group : t * part_rows + (i + 1) * group, :
                    ]
            return carry

        lax.fori_loop(0, states // group, right_chunk, 0)
        out_ref[s] = tn(m_ref[s], b_ref[...]) * scale


def finish(row_count, m, parts, right, rops):
    slots, states, cols = right.shape
    terms, site = rops.shape[0], rops.shape[1]
    return pl.pallas_call(
        functools.partial(finish_kernel, row_count),
        out_shape=jax.ShapeDtypeStruct((slots, m.shape[2], cols // row_count), F32),
        in_specs=[VM] * 4,
        out_specs=VM,
        scratch_shapes=[
            pltpu.VMEM((2, terms * 256 // row_count, 256), BF16),
            pltpu.VMEM((terms * states, cols // row_count), BF16),
        ],
        compiler_params=pltpu.CompilerParams(vmem_limit_bytes=40 * 2**20),
    )(m, parts, right, rops)


def solution(mesh):
    row_count, sec_count = mesh.shape["row"], mesh.shape["sec"]

    def on_device(left_block, right_block, left_ops, right_ops, charges, live_states, kept, start):
        left_all, arrived = exchange(row_count, sec_count, left_block, right_block)
        m, basis, part = chain(
            left_block.shape[0] * sec_count, left_all, arrived, left_ops, right_ops,
            charges, live_states, kept, start, left_block.shape[1],
        )
        m, parts = deliver(sec_count, m, part)
        return basis, finish(row_count, m, parts, right_block, right_ops)

    return jax.shard_map(
        on_device,
        mesh=mesh,
        in_specs=(P("sec", "row", None), P("sec", None, None), P(), P(), P(), P(), P(), P()),
        out_specs=(P("sec", "row", None), P("sec", None, "row")),
        check_vma=False,
    )
```

```python
import functools

import jax
import jax.numpy as jnp
from jax import lax
from jax.experimental import pallas as pl
from jax.experimental.pallas import tpu as pltpu
from jax.sharding import PartitionSpec as P

MESH = pl.DeviceIdType.MESH
HIGHEST = lax.Precision.HIGHEST
F32, BF16 = jnp.float32, jnp.bfloat16
chemical = 0.4
ITERS = 2
PANEL = 16
CHUNKS = 2
VM = pl.BlockSpec(memory_space=pltpu.VMEM)
SM = pl.BlockSpec(memory_space=pltpu.SMEM)


def nn(a, b, precision=None):
    return lax.dot_general(
        a, b, (((1,), (0,)), ((), ())), precision=precision, preferred_element_type=F32
    )


def nt(a, b, precision=None):
    return lax.dot_general(
        a, b, (((1,), (1,)), ((), ())), precision=precision, preferred_element_type=F32
    )


def tn(a, b, precision=None):
    return lax.dot_general(
        a, b, (((0,), (0,)), ((), ())), precision=precision, preferred_element_type=F32
    )


def split2(x):
    high = x.astype(BF16)
    return high, (x - high.astype(F32)).astype(BF16)


def split3(x):
    high, rest = x.astype(BF16), None
    rest = x - high.astype(F32)
    mid = rest.astype(BF16)
    return high, mid, (rest - mid.astype(F32)).astype(BF16)


def presplit_nn(parts, x):
    high, low = split2(x)
    both = nn(parts[0], jnp.concatenate([high, low], axis=1))
    width = x.shape[1]
    return both[:, :width] + both[:, width:] + nn(parts[1], high)


def nt3(a, b):
    ah, al = split2(a)
    bh, bl = split2(b)
    return nt(jnp.concatenate([ah, al, ah], axis=1), jnp.concatenate([bh, bh, bl], axis=1))


def iota(shape, dim):
    return lax.broadcasted_iota(jnp.int32, shape, dim)


def exchange_kernel(row_count, mask, left_ref, right_ref, left_out, right_out, send, recv):
    row, sec = lax.axis_index("row"), lax.axis_index("sec")
    rows = left_ref.shape[1]
    depth = right_ref.shape[1] // row_count

    def peer_row(distance):
        return (sec, jnp.bitwise_xor(row, distance))

    partner = (jnp.bitwise_xor(sec, mask), row)
    distances = []
    step = row_count // 2
    while step:
        distances.append(step)
        step //= 2
    barrier = pltpu.get_barrier_semaphore()
    for device in [partner] + [peer_row(d) for d in distances]:
        pl.semaphore_signal(barrier, inc=1, device_id=device, device_id_type=MESH)
    pl.semaphore_wait(barrier, 1 + len(distances))

    def left_at(owner):
        return left_out.at[:, pl.ds(pl.multiple_of(owner * rows, rows), rows), :]

    def right_at(ref, owner, c):
        size = depth // CHUNKS
        return ref.at[:, pl.ds(pl.multiple_of(owner * depth + c * size, size), size), :]

    copies = []

    def go(source, target, device):
        index = len(copies)
        copy = pltpu.make_async_remote_copy(
            src_ref=source, dst_ref=target, send_sem=send.at[index], recv_sem=recv.at[index],
            device_id=device, device_id_type=MESH,
        )
        copy.start()
        copies.append(copy)
        return copy

    taken = []

    def arrive(copy):
        if copy is not None and id(copy) not in taken:
            copy.wait_recv()
            taken.append(id(copy))

    pieces = [(row, c, go(*[right_at(ref, row, c) for ref in (right_ref, right_out)], partner)) for c in range(CHUNKS)]
    held = [(row, None)]
    for distance in distances:
        sent = []
        for owner, copy in held:
            arrive(copy)
            source = left_ref if copy is None else left_at(owner)
            sent.append(
                (jnp.bitwise_xor(owner, distance), go(source, left_at(owner), peer_row(distance)))
            )
        held = held + sent
    own = pl.ds(pl.multiple_of(row * rows, rows), rows)
    left_out[:, own, :] = left_ref[...]
    for distance in distances:
        sent = []
        for owner, c, copy in pieces:
            arrive(copy)
            block = right_at(right_out, owner, c)
            sent.append((jnp.bitwise_xor(owner, distance), c, go(block, block, peer_row(distance))))
        pieces = pieces + sent
    for copy in copies:
        copy.wait_send()
        arrive(copy)


def exchange(row_count, sec_count, left, right):
    slots, rows, states = left.shape
    count = row_count - 1 + CHUNKS * row_count
    return pl.pallas_call(
        functools.partial(exchange_kernel, row_count, sec_count // 2),
        out_shape=(
            jax.ShapeDtypeStruct((slots, rows * row_count, states), left.dtype),
            jax.ShapeDtypeStruct(right.shape, right.dtype),
        ),
        in_specs=[VM] * 2,
        out_specs=[VM] * 2,
        scratch_shapes=[pltpu.SemaphoreType.DMA((count,)), pltpu.SemaphoreType.DMA((count,))],
        compiler_params=pltpu.CompilerParams(collective_id=0, has_side_effects=True),
    )(left, right)


def spread(ops, row_of, col_of, same):
    site = ops.shape[0]
    pick_rows = (iota((row_of.shape[0], site), 1) == row_of).astype(BF16)
    pick_cols = (iota((site, col_of.shape[1]), 0) == col_of).astype(BF16)
    out = []
    for part in split2(ops):
        wide = nn(nn(pick_rows, part).astype(BF16), pick_cols)
        out.append(jnp.where(same, wide, 0.0).astype(BF16))
    return out


def inverse_factor(grams, s_ref, t_ref):
    size = grams[0].shape[0]
    slots = len(grams)
    eye = (iota((size, size), 0) == iota((size, size), 1)).astype(F32)
    for s in range(slots):
        s_ref[s] = grams[s]
        t_ref[s] = eye
    sub = iota((PANEL, size), 0)
    lane = iota((PANEL, size), 1)

    def panel(p, carry):
        base = pl.multiple_of(p * PANEL, PANEL)
        for s in range(slots):
            upper = s_ref[s, pl.ds(base, PANEL), :]
            lower = t_ref[s, pl.ds(base, PANEL), :]
            turned = pltpu.roll(upper, lax.rem(size - base, size), 1)
            cols = [jnp.broadcast_to(turned[:, c : c + 1], (PANEL, size)) for c in range(PANEL)]
            for j in range(PANEL):
                scale = lax.rsqrt(cols[j][j : j + 1, :])
                below = jnp.where(sub > j, cols[j] * scale, 0.0)
                at_j = sub == j

                def eliminate(x):
                    pivot = x[j : j + 1, :] * scale
                    return jnp.where(at_j, pivot, x - below * pivot)

                upper, lower = eliminate(upper), eliminate(lower)
                cols = [eliminate(c) if i > j else c for i, c in enumerate(cols)]
            t_ref[s, pl.ds(base, PANEL), :] = lower
            u3, l3 = split3(upper), split3(lower)
            later = lane >= base + PANEL
            m3 = [jnp.where(later, x.astype(F32), 0.0).astype(BF16) for x in u3]
            pairs = ((0, 0), (0, 1), (1, 0), (1, 1), (0, 2), (2, 0))
            lhs = jnp.concatenate([m3[i] for i, _ in pairs], axis=0)
            rhs = jnp.concatenate(
                [jnp.concatenate([u3[k], l3[k]], axis=1) for _, k in pairs], axis=0
            )
            change = tn(lhs, rhs)
            s_ref[s] = s_ref[s] - change[:, :size]
            t_ref[s] = t_ref[s] - change[:, size:]
        return carry

    lax.fori_loop(0, size // PANEL, panel, 0)


def chain_kernel(
    sector_count, left_ref, right_ref, lops_ref, rops_ref, charges_ref, live_ref, kept_ref,
    start_ref, m_out, u_out, part_out, at_ref, b_ref, kl_ref, kr_ref, ga_ref, gah_ref, gal_ref, gbh_ref,
    gbl_ref, s_ref, t_ref,
):
    slots, rows, states = left_ref.shape
    terms, site = lops_ref.shape[0], lops_ref.shape[1]
    cols = right_ref.shape[2]
    width = cols // site
    group = 256 // site
    block = group * site
    sec, row = lax.axis_index("sec"), lax.axis_index("row")
    homes = [sec * slots + s for s in range(slots)]
    mirrors = [lax.rem(h + sector_count // 2, sector_count) for h in homes]
    r0, c0 = iota((block, 1), 0), iota((1, block), 1)
    for t in range(terms):
        parts = spread(lops_ref[t].T, r0 % site, c0 % site, (r0 // site) == (c0 // site))
        for h in range(2):
            kl_ref[h, :, t * block : (t + 1) * block] = parts[h]
        parts = spread(rops_ref[t], r0 // group, c0 // group, (r0 % group) == (c0 % group))
        for h in range(2):
            kr_ref[h, t * block : (t + 1) * block, :] = parts[h]
    for s in range(slots):
        limit = live_ref[homes[s]] * site

        def left_chunk(c, carry):
            base = pl.multiple_of(c * block, block)
            piece = left_ref[s, pl.ds(base, block), :]
            piece = jnp.where(iota((block, states), 0) + base < limit, piece.astype(F32), 0.0)
            turned = piece.T.astype(BF16)
            out = nn(turned, kl_ref[0]) + nn(turned, kl_ref[1])
            for t in range(terms):
                at_ref[s, t * states : (t + 1) * states, pl.ds(base, block)] = out[
                    :, t * block : (t + 1) * block
                ].astype(BF16)
            return carry

        lax.fori_loop(0, rows // block, left_chunk, 0)

        def right_chunk(c, carry):
            base = pl.multiple_of(c * group, group)
            piece = right_ref[s, pl.ds(base, group), :]
            stack = jnp.concatenate([piece[:, j * width : (j + 1) * width] for j in range(site)], axis=0)
            out = (nn(kr_ref[0], stack) + nn(kr_ref[1], stack)).astype(BF16)
            for t in range(terms):
                for i in range(site):
                    b_ref[
                        s, pl.ds(t * states + base, group), i * width : (i + 1) * width
                    ] = out[t * block + i * group : t * block + (i + 1) * group, :]
            return carry

        lax.fori_loop(0, states // group, right_chunk, 0)
        gram = nt(at_ref[s], at_ref[s])
        ga_ref[s] = gram
        gah_ref[s], gal_ref[s] = split2(gram)
        gbh_ref[s], gbl_ref[s] = split2(nt(b_ref[s], b_ref[s]))

    bond = terms * states
    weights = [
        jnp.exp(jnp.full((1, states), charges_ref[m], jnp.int32).astype(F32) * (-chemical))
        for m in mirrors
    ]
    coef = []
    for s in range(slots):
        wanted = start_ref[pl.ds(homes[s], 1), :]
        coef.append((iota((bond, wanted.shape[1]), 0) == wanted).astype(F32))
    for round_index in range(ITERS + 1):
        if round_index < ITERS:
            image = [presplit_nn((gah_ref[s], gal_ref[s]), coef[s]) for s in range(slots)]
        else:
            image = [nn(ga_ref[s], coef[s], HIGHEST) for s in range(slots)]
        inverse_factor([tn(coef[s], image[s], HIGHEST) for s in range(slots)], s_ref, t_ref)
        image = [nt3(image[s], t_ref[s]) for s in range(slots)]
        if round_index < ITERS:
            coef = [
                presplit_nn((gbh_ref[s], gbl_ref[s]), image[s]) * (weights[s] * weights[s])
                for s in range(slots)
            ]
        else:
            coef = [nt3(coef[s], t_ref[s]) for s in range(slots)]
    local_rows = u_out.shape[1]
    total = jnp.zeros((8, states), F32)
    for s in range(slots):
        keep = iota((bond, coef[s].shape[1]), 1) < kept_ref[mirrors[s]]
        out = jnp.where(keep, image[s] * weights[s], 0.0)
        m_out[s] = out.astype(BF16)
        per = out * presplit_nn((gbh_ref[s], gbl_ref[s]), out)
        total = total + jnp.sum(per.reshape(bond // 8, 8, per.shape[1]), axis=0)
        high, low = split2(jnp.where(keep, coef[s], 0.0))
        here = at_ref[s, :, pl.ds(pl.multiple_of(row * local_rows, local_rows), local_rows)]
        u_out[s] = tn(here, high) + tn(here, low)
    part_out[...] = total


def chain(sector_count, left, right, lops, rops, charges, live, kept, start, local_rows):
    slots, rows, states = left.shape
    terms, site = lops.shape[0], lops.shape[1]
    cols, bond, keep = right.shape[2], terms * states, start.shape[1]
    block = 256
    return pl.pallas_call(
        functools.partial(chain_kernel, sector_count),
        out_shape=(
            jax.ShapeDtypeStruct((slots, bond, keep), BF16),
            jax.ShapeDtypeStruct((slots, local_rows, keep), F32),
            jax.ShapeDtypeStruct((8, keep), F32),
        ),
        in_specs=[VM] * 4 + [SM] * 3 + [VM],
        out_specs=[VM] * 3,
        scratch_shapes=[
            pltpu.VMEM((slots, bond, rows), BF16),
            pltpu.VMEM((slots, bond, cols), BF16),
            pltpu.VMEM((2, block, terms * block), BF16),
            pltpu.VMEM((2, terms * block, block), BF16),
            pltpu.VMEM((slots, bond, bond), F32),
            pltpu.VMEM((slots, bond, bond), BF16),
            pltpu.VMEM((slots, bond, bond), BF16),
            pltpu.VMEM((slots, bond, bond), BF16),
            pltpu.VMEM((slots, bond, bond), BF16),
            pltpu.VMEM((slots, keep, keep), F32),
            pltpu.VMEM((slots, keep, keep), F32),
        ],
        compiler_params=pltpu.CompilerParams(vmem_limit_bytes=56 * 2**20),
    )(left, right, lops, rops, charges, live, kept, start)


def deliver_kernel(row_count, sec_count, m_ref, part_ref, m_out, parts_out, m_send, m_recv, send, recv):
    row, sec = lax.axis_index("row"), lax.axis_index("sec")
    depth = m_ref.shape[1] // row_count
    distances = []
    step = row_count // 2
    while step:
        distances.append(step)
        step //= 2
    barrier = pltpu.get_barrier_semaphore()
    for d in range(1, sec_count):
        pl.semaphore_signal(
            barrier, inc=1, device_id=(jnp.bitwise_xor(sec, d), row), device_id_type=MESH
        )
    for d in distances:
        pl.semaphore_signal(
            barrier, inc=1, device_id=(sec, jnp.bitwise_xor(row, d)), device_id_type=MESH
        )
    pl.semaphore_wait(barrier, sec_count - 1 + len(distances))

    def part_of(ref, owner):
        return ref.at[:, pl.ds(pl.multiple_of(owner * depth, depth), depth), :]

    copies, taken = [], []

    def go(source, target, device):
        index = len(copies)
        copy = pltpu.make_async_remote_copy(
            src_ref=source, dst_ref=target, send_sem=m_send.at[index], recv_sem=m_recv.at[index],
            device_id=device, device_id_type=MESH,
        )
        copy.start()
        copies.append(copy)
        return copy

    def arrive(copy):
        if id(copy) not in taken:
            copy.wait_recv()
            taken.append(id(copy))

    partner = (jnp.bitwise_xor(sec, sec_count // 2), row)
    held = [(row, go(part_of(m_ref, row), part_of(m_out, row), partner))]
    small = []
    for d in range(1, sec_count):
        copy = pltpu.make_async_remote_copy(
            src_ref=part_ref, dst_ref=parts_out.at[d], send_sem=send.at[d], recv_sem=recv.at[d],
            device_id=(jnp.bitwise_xor(sec, d), row), device_id_type=MESH,
        )
        copy.start()
        small.append(copy)
    parts_out[0] = part_ref[...]
    for distance in distances:
        sent = []
        for owner, copy in held:
            arrive(copy)
            block = part_of(m_out, owner)
            peer = (sec, jnp.bitwise_xor(row, distance))
            sent.append((jnp.bitwise_xor(owner, distance), go(block, block, peer)))
        held = held + sent
    for copy in small:
        copy.wait()
    for copy in copies:
        copy.wait_send()
        arrive(copy)


def deliver(row_count, sec_count, m, part):
    return pl.pallas_call(
        functools.partial(deliver_kernel, row_count, sec_count),
        out_shape=(
            jax.ShapeDtypeStruct(m.shape, m.dtype),
            jax.ShapeDtypeStruct((sec_count,) + part.shape, part.dtype),
        ),
        in_specs=[VM] * 2,
        out_specs=[VM] * 2,
        scratch_shapes=[
            pltpu.SemaphoreType.DMA((row_count,)),
            pltpu.SemaphoreType.DMA((row_count,)),
            pltpu.SemaphoreType.DMA((sec_count,)),
            pltpu.SemaphoreType.DMA((sec_count,)),
        ],
        compiler_params=pltpu.CompilerParams(collective_id=1, has_side_effects=True),
    )(m, part)


def finish_kernel(row_count, m_ref, parts_ref, right_ref, rops_ref, out_ref, kr_ref, b_ref):
    slots, states, cols = right_ref.shape
    terms, site = rops_ref.shape[0], rops_ref.shape[1]
    width = cols // site
    group = 256 // site
    block = group * site
    here = site // row_count
    part_rows = here * group
    row = lax.axis_index("row")
    r0, c0 = iota((part_rows, 1), 0), iota((1, block), 1)
    for t in range(terms):
        parts = spread(
            rops_ref[t], row * here + r0 // group, c0 // group, (r0 % group) == (c0 % group)
        )
        for h in range(2):
            kr_ref[h, t * part_rows : (t + 1) * part_rows, :] = parts[h]
    total = jnp.sum(jnp.sum(parts_ref[...], axis=0), keepdims=True)
    scale = 1.0 / jnp.sqrt(total)
    for s in range(slots):
        def right_chunk(c, carry):
            base = pl.multiple_of(c * group, group)
            piece = right_ref[s, pl.ds(base, group), :]
            stack = jnp.concatenate([piece[:, j * width : (j + 1) * width] for j in range(site)], axis=0)
            out = (nn(kr_ref[0], stack) + nn(kr_ref[1], stack)).astype(BF16)
            for t in range(terms):
                for i in range(here):
                    b_ref[pl.ds(t * states + base, group), i * width : (i + 1) * width] = out[
                        t * part_rows + i * group : t * part_rows + (i + 1) * group, :
                    ]
            return carry

        lax.fori_loop(0, states // group, right_chunk, 0)
        out_ref[s] = tn(m_ref[s], b_ref[...]) * scale


def finish(row_count, m, parts, right, rops):
    slots, states, cols = right.shape
    terms, site = rops.shape[0], rops.shape[1]
    return pl.pallas_call(
        functools.partial(finish_kernel, row_count),
        out_shape=jax.ShapeDtypeStruct((slots, m.shape[2], cols // row_count), F32),
        in_specs=[VM] * 4,
        out_specs=VM,
        scratch_shapes=[
            pltpu.VMEM((2, terms * 256 // row_count, 256), BF16),
            pltpu.VMEM((terms * states, cols // row_count), BF16),
        ],
        compiler_params=pltpu.CompilerParams(vmem_limit_bytes=40 * 2**20),
    )(m, parts, right, rops)


def solution(mesh):
    row_count, sec_count = mesh.shape["row"], mesh.shape["sec"]

    def on_device(left_block, right_block, left_ops, right_ops, charges, live_states, kept, start):
        left_all, arrived = exchange(row_count, sec_count, left_block, right_block)
        m, basis, part = chain(
            left_block.shape[0] * sec_count, left_all, arrived, left_ops, right_ops,
            charges, live_states, kept, start, left_block.shape[1],
        )
        m, parts = deliver(row_count, sec_count, m, part)
        return basis, finish(row_count, m, parts, right_block, right_ops)

    return jax.shard_map(
        on_device,
        mesh=mesh,
        in_specs=(P("sec", "row", None), P("sec", None, None), P(), P(), P(), P(), P(), P()),
        out_specs=(P("sec", "row", None), P("sec", None, "row")),
        check_vma=False,
    )
```
